32 devices in a mesh: real: 2 (over y), rows: 4 (over z), orb: 4 (over x, core).
Axes of the slice: x: 2, y: 2, z: 4, core: 2. Of those that a mesh axis runs over, the one named last changes fastest.
Arguments:
- occupied: bfloat16 [2, 16, 256, 1024], P(None, ('real', 'rows'), None, 'orb'), parts along dimension 1, may hold values from -2.5 to 2.5
- disorder: int32 [16, 256], P(('real', 'rows')), parts along dimension 0, may hold values from -8 to 8
- region_cols: int32 [32], replicated, may hold values from 0 to 255, as said below
- cheb_coef: float32 [2, 8], replicated, may hold values from -0.6 to 0.6
- prior_corr: bfloat16 [2, 512, 256], P(None, ('real', 'rows'), 'orb'), parts along dimension 1, may hold values from -6 to 6
Outputs:
- correlation: float32 [2, 512, 256], P(None, ('real', 'rows'), 'orb'), parts along dimension 1
The draws below stay inside these ranges and needn't reach their ends.
There are 2 independent parts, one for each index of `real`. The reference program is written for one: setup_inputs(seed, part) draws one part's arguments, and reference() takes and returns one part's arrays. A program takes and returns all parts, laid end to end along the dimension named above; an argument that names none is the same for every part. Nothing has to cross between parts.
Inputs may be any that keep to these rules, and one draw needn't show every extreme that they name: `region_cols`: 32 distinct columns; columns 0 and 255 are always among them.
All inputs are finite; a program needn't handle non-finite values.
Results may differ from the reference program's by a relative error of at most 0.0033.
Values may be sent and summed in bfloat16 or wider, within the bound.
A program may use at most 64 MiB of HBM per device.

```python
import jax
import jax.numpy as jnp
from jax import lax

LX = 256
M = 1024
ACOLS = 32
KTERMS = 8
LY = 8
NA = 256


def draw_region_cols(key, part):
    inner = jax.random.permutation(jax.random.fold_in(key, 11), LX - 2)[:ACOLS - 2] + 1
    columns = jnp.concatenate([jnp.array([0, LX - 1], jnp.int32), inner.astype(jnp.int32)])
    shuffle = jax.random.permutation(jax.random.fold_in(key, 12), ACOLS)
    return columns[shuffle]


def place_ends(drawn, key, low, largest):
    dims = drawn.shape
    place = [jax.random.randint(jax.random.fold_in(key, axis), (), 0, dims[axis]) for axis in range(len(dims))]
    drawn = drawn.at[tuple(place)].set(low)
    longest = dims.index(max(dims))
    place[longest] = (place[longest] + 1) % dims[longest]
    return drawn.at[tuple(place)].set(largest)


def level_of(rng, dims, pieces, smallest, high):
    def one(dim, blocks):
        steps = jax.random.uniform(jax.random.fold_in(jax.random.fold_in(rng, 6), dim), (blocks,), jnp.float32, smallest / len(pieces), high / len(pieces))
        return jnp.repeat(jnp.exp(steps), dims[dim] // blocks).reshape((-1,) + (1,) * (len(dims) - dim - 1))

    loudness = one(*pieces[0])
    for cut in pieces[1:]:
        loudness = loudness * one(*cut)
    return loudness


def centred(key, extent, width, most, shards=(), kind=jnp.bfloat16):
    drawn = width * jax.random.normal(key, extent, jnp.float32)
    if shards:
        drawn = drawn * level_of(key, extent, shards, -0.22, 0.18)
    return jnp.clip(drawn, -most, most).astype(kind)


def setup_inputs(seed: int = 0, part: int = 0) -> dict:
    key_list = jax.random.split(jax.random.key(seed), 6)
    own_keys = jax.random.split(jax.random.fold_in(key_list[5], part), 6)
    occupied = centred(own_keys[0], (2, LY, LX, M), 0.18, 2.5, ((1, 4), (3, 4)))
    disorder = place_ends(jax.random.randint(own_keys[1], (LY, LX), -8, 9), jax.random.fold_in(own_keys[1], 1), -8, 8).astype(jnp.int32)
    region_cols = draw_region_cols(jax.random.fold_in(key_list[5], 71), part)
    cheb_coef = jnp.clip(jax.random.uniform(key_list[3], (2, KTERMS), jnp.float32, -0.6, 0.6), -0.6, 0.6)
    prior_corr = centred(own_keys[4], (2, NA, NA), 1.0, 6.0, ((1, 4), (2, 4)))
    return {"occupied": occupied, "disorder": disorder, "region_cols": region_cols, "cheb_coef": cheb_coef, "prior_corr": prior_corr}


HOP_SCALE = 5.25
LEVEL_STEP = 0.125


def apply_hop(state, onsite):
    neighbours = jnp.roll(state, -1, 1) + jnp.roll(state, 1, 1) + jnp.roll(state, -1, 2) + jnp.roll(state, 1, 2)
    return (onsite[None, :, :, None] * state - neighbours) / HOP_SCALE


def rotate(picked):
    return jnp.stack([-picked[1], picked[0]])


def reference(occupied, disorder, region_cols, cheb_coef, prior_corr):
    onsite = disorder.astype(jnp.float32) * LEVEL_STEP
    current = occupied.astype(jnp.float32)

    def select_cols(state):
        return jnp.take(state, region_cols, axis=2)

    picked = select_cols(current)
    summed = cheb_coef[0, 0] * picked + cheb_coef[1, 0] * rotate(picked)
    previous = current
    for degree in range(1, KTERMS):
        applied = apply_hop(current, onsite)
        following = applied if degree == 1 else 2.0 * applied - previous
        previous, current = current, following
        picked = select_cols(current)
        summed = summed + (cheb_coef[0, degree] * picked + cheb_coef[1, degree] * rotate(picked))
    evolved = summed.astype(jnp.bfloat16).reshape(2, LY * ACOLS, M)
    evolved_wide = evolved.astype(jnp.float32)
    block_rows = 8 * ACOLS

    def row_block(index):
        part = lax.dynamic_slice_in_dim(evolved_wide, index * block_rows, block_rows, 1)
        products = jnp.einsum("cim,djm->cdij", part, evolved_wide)
        return jnp.stack([products[0, 0] + products[1, 1], products[1, 0] - products[0, 1]])

    blocks = lax.map(row_block, jnp.arange(LY // 8, dtype=jnp.int32))
    tiles = jnp.transpose(blocks, (1, 0, 2, 3)).reshape(2, LY * ACOLS, LY * ACOLS)
    return prior_corr.astype(jnp.float32) + tiles
```

```python
import functools

import jax
import jax.numpy as jnp
from jax import lax
from jax.experimental import pallas as pl
from jax.experimental.pallas import tpu as pltpu
from jax.sharding import PartitionSpec as P

HOP_SCALE = 5.25
LEVEL_STEP = 0.125


def padded_2(cells, sides, width):
    for axis, dim in sides:
        count = lax.axis_size(axis)
        head = lax.slice_in_dim(cells, 0, width, axis=dim)
        tail = lax.slice_in_dim(cells, cells.shape[dim] - width, cells.shape[dim], axis=dim)
        cells = jnp.concatenate(
            [
                lax.ppermute(tail, axis, [(i, (i + 1) % count) for i in range(count)]),
                cells,
                lax.ppermute(head, axis, [((i + 1) % count, i) for i in range(count)]),
            ],
            axis=dim,
        )
    return cells


def apply_rows(padded, onsite):
    middle = padded[:, 1:-1]
    neighbours = padded[:, 2:] + padded[:, :-2] + jnp.roll(middle, -1, 2) + jnp.roll(middle, 1, 2)
    return (onsite[None, :, :, None] * middle - neighbours) / HOP_SCALE


def rotate(picked):
    return jnp.stack([-picked[1], picked[0]])


def combine_pairs(products):
    return jnp.stack([products[0, 0] + products[1, 1], products[1, 0] - products[0, 1]])


def shards(occupied, disorder, region_cols, cheb_coef, prior_corr):
    band_rows = occupied.shape[1]
    term_count = cheb_coef.shape[1]
    current = occupied.astype(jnp.float32)

    def contribution(state, degree):
        picked = jnp.take(state, region_cols, axis=2)
        return cheb_coef[0, degree] * picked + cheb_coef[1, degree] * rotate(picked)

    summed = contribution(current, 0)
    previous = current
    onsite = disorder.astype(jnp.float32) * LEVEL_STEP
    for degree in range(1, term_count):
        padded = padded_2(current, (("rows", 1),), 1)
        applied = apply_rows(padded, onsite)
        following = applied if degree == 1 else 2.0 * applied - previous
        previous, current = (current, following)
        summed = summed + contribution(current, degree)
    tile_rows = band_rows * region_cols.shape[0]
    evolved = summed.astype(jnp.bfloat16).reshape(2, tile_rows, summed.shape[3])
    row_panel = lax.all_gather(evolved, "orb", axis=2, tiled=True)
    column_all = lax.all_gather(evolved, "rows", axis=1, tiled=True)
    column_panel = lax.all_to_all(column_all, "orb", split_axis=1, concat_axis=2, tiled=True)
    products = jnp.einsum(
        "cim,djm->cdij", row_panel, column_panel, preferred_element_type=jnp.float32
    )
    tile_sum = combine_pairs(products)
    return prior_corr.astype(jnp.float32) + tile_sum


LANES = 128
FRAME = 16
MESH = pl.DeviceIdType.MESH


def quench_kernel(
    row_count, occupied, disorder, region_cols, cheb_coef, out,
    fields, turned, levels, hot, window, picks, operator, product, kept, leaving,
    crossed, outgoing, incoming, columns, weights,
    load_sem, level_send, level_recv, field_send, field_recv,
    cross_send, cross_recv, block_send, block_recv,
):
    r = lax.axis_index("rows")
    o = lax.axis_index("orb")
    g = o % 2
    x = o // 2
    band, width = disorder.shape
    height = band * row_count
    terms = cheb_coef.shape[1]
    reach = terms - 1
    acols = region_cols.shape[0]
    tile = out.shape[1]
    chips = 2 * row_count
    mine = 2 * r + x
    half = row_count // 2
    side = r // half
    place = r % half
    pair = r + 1 - 2 * place
    across = (r + half) % row_count
    owner = g == side
    spots = 2 * LANES

    def remote(src, dst, send, recv, row, orb):
        return pltpu.make_async_remote_copy(
            src_ref=src, dst_ref=dst, send_sem=send, recv_sem=recv,
            device_id={"rows": row, "orb": orb}, device_id_type=MESH,
        )

    barrier = pltpu.get_barrier_semaphore()

    def greet(row, orb):
        pl.semaphore_signal(
            barrier, inc=1, device_id={"rows": row, "orb": orb}, device_id_type=MESH
        )

    has_left, has_right = r > 0, r < row_count - 1
    pl.when(has_left)(lambda: greet((r + row_count - 1) % row_count, o))
    pl.when(has_right)(lambda: greet((r + 1) % row_count, o))
    for k in range(1, 4):
        greet(r, (o + k) % 4)

    def chunk(i, which):
        return occupied.at[:, i, :, pl.ds(pl.multiple_of(which * LANES, LANES), LANES)]

    loads = [
        pltpu.make_async_copy(disorder, levels.at[r], load_sem.at[0]),
        pltpu.make_async_copy(region_cols, columns, load_sem.at[1]),
        pltpu.make_async_copy(cheb_coef, weights, load_sem.at[2]),
    ]
    for load in loads:
        load.start()
    own_loads = [
        pltpu.make_async_copy(chunk(i, place), fields.at[0, i], field_recv.at[0, i])
        for i in range(band)
    ]
    for load in own_loads:
        load.start()
    for load in loads:
        load.wait()

    pl.semaphore_wait(
        barrier, 3 + jnp.where(has_left, 1, 0) + jnp.where(has_right, 1, 0)
    )

    def level_copy(first, count, way, kind, row):
        part = levels.at[pl.ds(first, count)]
        return remote(part, part, level_send.at[kind], level_recv.at[way], row, o)

    to_left = functools.partial(level_copy, r, 1, 1, 0, (r + row_count - 1) % row_count)
    to_right = functools.partial(level_copy, r, 1, 0, 1, (r + 1) % row_count)
    pl.when(has_left)(lambda: to_left().start())
    pl.when(has_right)(lambda: to_right().start())

    def field_copy(i):
        return remote(
            chunk(i, 1 - place), fields.at[1, i], field_send.at[i],
            field_recv.at[1, i], pair, o,
        )

    for i in range(band):
        field_copy(i).start()

    lane = lax.broadcasted_iota(jnp.int32, (1, LANES), 1)
    cols = jnp.zeros((1, LANES), jnp.int32)
    for a in range(acols):
        cols = jnp.where(lane % acols == a, columns[a], cols)
    offset = lax.broadcasted_iota(jnp.int32, (width, LANES), 0) - cols + reach
    offset = jnp.where(offset < 0, offset + width, offset)
    offset = jnp.where(offset >= width, offset - width, offset)
    for d in range(1, 2 * reach):
        hot[d - 1] = jnp.where(offset == d, 1.0, 0.0).astype(jnp.bfloat16)

    first = cols - reach
    first = jnp.where(first < 0, first + width, first)
    first = jnp.concatenate([first, first], axis=1)
    slide = jnp.broadcast_to(first % FRAME, (2 * FRAME, spots))
    strip = jnp.broadcast_to(first // FRAME, (FRAME, spots))
    strips = width // FRAME
    for j in range(strips):
        picks[j] = jnp.where(strip == j, 1.0, 0.0).astype(jnp.bfloat16)

    def turn(slot, i):
        k = band * slot + i
        for part in range(2):
            turned[part * LANES : (part + 1) * LANES, k * width : (k + 1) * width] = (
                fields[slot, i, part].T
            )

    for i in range(band):
        own_loads[i].wait()
        turn(0, i)

    @pl.when(has_left)
    def _():
        level_copy((r + row_count - 1) % row_count, 1, 0, 1, r).wait_recv()

    @pl.when(has_right)
    def _():
        level_copy((r + 1) % row_count, 1, 1, 0, r).wait_recv()

    middle = (r > 0) & (r < row_count - 1)
    behind = (row_count - 1) * side
    both_far = functools.partial(level_copy, half * side, half, 2, 2, (row_count - 1) * (1 - side))
    one_near = functools.partial(level_copy, behind, 1, 2, 3, row_count - 1 - r)

    @pl.when(middle)
    def _():
        both_far().start()
        one_near().start()
        level_copy((row_count - 1) * (1 - side), 1, 2, 3, r).wait_recv()

    @pl.when(jnp.logical_not(middle))
    def _():
        level_copy(half * (1 - side), half, 2, 2, r).wait_recv()

    onsite = jnp.concatenate([levels[k] for k in range(row_count)], axis=0)
    onsite = (onsite.astype(jnp.float32) * LEVEL_STEP).astype(jnp.bfloat16)

    local_levels = {}
    for d in range(1, 2 * reach):
        here = jnp.dot(onsite, hot[d - 1], preferred_element_type=jnp.float32)
        local_levels[d] = jnp.concatenate([here, here], axis=1)

    lane = lax.broadcasted_iota(jnp.int32, (height, spots), 1)
    row_id = lax.broadcasted_iota(jnp.int32, (height, spots), 0)
    start = jnp.where(row_id == lane // acols, 1.0, 0.0)
    previous, current = {}, {reach: start}
    real = {reach: weights[0, 0] * start}
    imag = {reach: weights[1, 0] * start}
    for degree in range(1, terms):
        following = {}
        for d in range(reach - degree, reach + degree + 1):
            total = None
            if d in current:
                here = current[d]
                total = local_levels[d] * here - (
                    pltpu.roll(here, 1, 0) + pltpu.roll(here, height - 1, 0)
                )
            for beside in (d - 1, d + 1):
                if beside in current:
                    there = current[beside]
                    total = -there if total is None else total - there
            value = total * ((1.0 if degree == 1 else 2.0) / HOP_SCALE)
            if d in previous:
                value = value - previous[d]
            following[d] = value
            more_real = weights[0, degree] * value
            more_imag = weights[1, degree] * value
            real[d] = real[d] + more_real if d in real else more_real
            imag[d] = imag[d] + more_imag if d in imag else more_imag
        previous, current = current, following
    for part, parts in ((0, real), (1, imag)):
        for d in range(FRAME):
            rows = pl.ds((part * FRAME + d) * height, height)
            value = parts[d] if d in parts else jnp.zeros((height, spots), jnp.float32)
            window[0, rows, :] = value[:, :LANES]
            window[1, rows, :] = value[:, LANES:]

    def expand(slot, i):
        k = band * slot + i
        where = place if slot == 0 else 1 - place
        y = band * (half * side + where) + i
        for part in range(2):
            rows = pl.ds(part * FRAME * height + y, FRAME, stride=height)
            bare = jnp.concatenate([window[0, rows, :], window[1, rows, :]], axis=1)
            frame = jnp.concatenate([bare, jnp.zeros_like(bare)], axis=0)
            step = 1
            while step < FRAME:
                moved = pltpu.roll(frame, step, 0)
                frame = jnp.where((slide & step) != 0, moved, frame)
                step *= 2
            high = frame.astype(jnp.bfloat16)
            low = (frame - high.astype(jnp.float32)).astype(jnp.bfloat16)
            for kind, value in ((0, high), (1, low)):
                upper, lower = value[:FRAME], value[FRAME:]
                for j in range(strips):
                    operator[
                        kind, k * width + j * FRAME : k * width + (j + 1) * FRAME,
                        part * spots : (part + 1) * spots,
                    ] = upper * picks[j] + lower * picks[(j - 1) % strips]

    def applied(slot):
        rows = slice(slot * band * width, (slot + 1) * band * width)
        return jnp.dot(
            turned[:, rows], operator[0, rows, :], preferred_element_type=jnp.float32
        ) + jnp.dot(turned[:, rows], operator[1, rows, :], preferred_element_type=jnp.float32)

    for i in range(band):
        expand(0, i)
    product[...] = applied(0)
    for i in range(band):
        expand(1, i)
    for i in range(band):
        remote(
            fields.at[1, i], fields.at[1, i], field_send.at[i], field_recv.at[1, i], pair, o
        ).wait_recv()
        turn(1, i)
    total = product[...] + applied(1)
    sum0 = total[:LANES, :spots] - total[LANES:, spots:]
    sum1 = total[LANES:, :spots] + total[:LANES, spots:]

    def cross_copy():
        return remote(leaving, crossed, cross_send, cross_recv, across, o)

    def block_copy(k, part, slot):
        to = (mine + k) % chips
        place_of = 2 * to + part
        return remote(
            outgoing.at[place_of], incoming.at[slot], block_send.at[2 * k + part],
            block_recv.at[slot], to // 2, 2 * (to % 2) + part,
        )

    def mate_copy():
        return remote(
            outgoing.at[2 * mine + 1 - g], incoming.at[mine], block_send.at[0],
            block_recv.at[mine], r, 2 * x + 1 - g,
        )

    @pl.when(jnp.logical_not(owner))
    def _():
        leaving[0] = sum0.astype(jnp.bfloat16)
        leaving[1] = sum1.astype(jnp.bfloat16)
        cross_copy().start()

    @pl.when(owner)
    def _():
        kept[0] = sum0
        kept[1] = sum1
        cross_copy().wait_recv()
        evolved = [
            (kept[part] + crossed[part].astype(jnp.float32)).astype(jnp.bfloat16).T
            for part in range(2)
        ]
        left = jnp.concatenate([evolved[0], evolved[1]], axis=1)
        flipped = jnp.concatenate([-evolved[1], evolved[0]], axis=1)
        rights = []
        for column in range(4):
            rows = slice(column * tile, (column + 1) * tile)
            rights.append(left[rows])
            rights.append(flipped[rows])
        blocks = lax.dot_general(
            left, jnp.concatenate(rights, axis=0), (((1,), (1,)), ((), ())),
            preferred_element_type=jnp.float32,
        ).astype(jnp.bfloat16)
        for row in range(row_count):
            for column in range(4):
                outgoing[4 * row + column] = blocks[
                    row * tile : (row + 1) * tile, column * LANES : (column + 1) * LANES
                ]
        for k in range(chips - 1, 0, -1):
            for part in range(2):
                block_copy(k, part, mine).start()
        mate_copy().start()
        incoming[mine] = outgoing[2 * mine + g]

    pl.when(jnp.logical_not(owner))(lambda: mate_copy().wait_recv())
    total = incoming[mine].astype(jnp.float32)
    for k in range(1, chips):
        slot = (mine + chips - k) % chips
        block_copy(k, 0, slot).wait_recv()
        total = total + incoming[slot].astype(jnp.float32)
    out[0] = total[:, :tile]
    out[1] = total[:, tile:]

    pl.when(has_left)(lambda: to_left().wait_send())
    pl.when(has_right)(lambda: to_right().wait_send())

    @pl.when(middle)
    def _():
        both_far().wait_send()
        one_near().wait_send()

    for i in range(band):
        field_copy(i).wait_send()
    pl.when(jnp.logical_not(owner))(lambda: cross_copy().wait_send())

    @pl.when(owner)
    def _():
        mate_copy().wait_send()
        for k in range(1, chips):
            for part in range(2):
                block_copy(k, part, mine).wait_send()


def fused_step(row_count, occupied, disorder, region_cols, cheb_coef, prior_corr):
    band, width = disorder.shape
    terms = cheb_coef.shape[1]
    tile = prior_corr.shape[1]
    height = band * row_count
    chips = 2 * row_count
    half = row_count // 2
    spots = 2 * LANES
    dma = pltpu.SemaphoreType.DMA
    anywhere = pl.BlockSpec(memory_space=pl.ANY)
    corr = pl.pallas_call(
        functools.partial(quench_kernel, row_count),
        out_shape=pltpu.VMEM(prior_corr.shape, jnp.float32),
        in_specs=[anywhere] * 4,
        out_specs=pl.BlockSpec(memory_space=pltpu.VMEM),
        scratch_shapes=[
            pltpu.VMEM((2, band, 2, width, LANES), jnp.bfloat16),
            pltpu.VMEM((2 * LANES, height // 2 * width), jnp.bfloat16),
            pltpu.VMEM((row_count, band, width), jnp.int32),
            pltpu.VMEM((2 * terms - 3, width, LANES), jnp.bfloat16),
            pltpu.VMEM((2, 2 * FRAME * height, LANES), jnp.float32),
            pltpu.VMEM((width // FRAME, FRAME, spots), jnp.bfloat16),
            pltpu.VMEM((2, height // 2 * width, 2 * spots), jnp.bfloat16),
            pltpu.VMEM((2 * LANES, 2 * spots), jnp.float32),
            pltpu.VMEM((2, LANES, spots), jnp.float32),
            pltpu.VMEM((2, LANES, spots), jnp.bfloat16),
            pltpu.VMEM((2, LANES, spots), jnp.bfloat16),
            pltpu.VMEM((2 * chips, tile, LANES), jnp.bfloat16),
            pltpu.VMEM((chips, tile, LANES), jnp.bfloat16),
            pltpu.SMEM(region_cols.shape, jnp.int32),
            pltpu.SMEM(cheb_coef.shape, jnp.float32),
            dma((3,)),
            dma((4,)),
            dma((3,)),
            dma((band,)),
            dma((2, band)),
            dma,
            dma,
            dma((2 * chips,)),
            dma((chips,)),
        ],
        compiler_params=pltpu.CompilerParams(collective_id=0, has_side_effects=True),
    )(occupied, disorder, region_cols, cheb_coef)
    return prior_corr.astype(jnp.float32) + corr


def local_step(row_count, orb_count, occupied, disorder, region_cols, cheb_coef, prior_corr):
    band, width, orbitals = occupied.shape[1:]
    terms = cheb_coef.shape[1]
    height = band * row_count
    sites = height * region_cols.shape[0]
    fused = (
        orb_count == 4
        and row_count == 4
        and sites == 2 * LANES
        and 2 * orbitals == row_count * LANES
        and orbitals == 2 * LANES
        and height % 8 == 0
        and width % LANES == 0
        and width >= 2 * FRAME
        and 2 * terms <= FRAME
        and LANES % region_cols.shape[0] == 0
        and prior_corr.shape[1:] == (LANES // 2, LANES // 2)
    )
    if fused:
        return fused_step(row_count, occupied, disorder, region_cols, cheb_coef, prior_corr)
    return shards(occupied, disorder, region_cols, cheb_coef, prior_corr)


def solution(mesh):
    return jax.shard_map(
        functools.partial(local_step, mesh.shape["rows"], mesh.shape["orb"]),
        mesh=mesh,
        in_specs=(
            P(None, ("real", "rows"), None, "orb"),
            P(("real", "rows"), None),
            P(),
            P(),
            P(None, ("real", "rows"), "orb"),
        ),
        out_specs=P(None, ("real", "rows"), "orb"),
        check_vma=False,
    )
```

```python
import functools

import jax
import jax.numpy as jnp
from jax import lax
from jax.experimental import pallas as pl
from jax.experimental.pallas import tpu as pltpu
from jax.sharding import PartitionSpec as P

HOP_SCALE = 5.25
LEVEL_STEP = 0.125


def padded_2(cells, sides, width):
    for axis, dim in sides:
        count = lax.axis_size(axis)
        head = lax.slice_in_dim(cells, 0, width, axis=dim)
        tail = lax.slice_in_dim(cells, cells.shape[dim] - width, cells.shape[dim], axis=dim)
        cells = jnp.concatenate(
            [
                lax.ppermute(tail, axis, [(i, (i + 1) % count) for i in range(count)]),
                cells,
                lax.ppermute(head, axis, [((i + 1) % count, i) for i in range(count)]),
            ],
            axis=dim,
        )
    return cells


def apply_rows(padded, onsite):
    middle = padded[:, 1:-1]
    neighbours = padded[:, 2:] + padded[:, :-2] + jnp.roll(middle, -1, 2) + jnp.roll(middle, 1, 2)
    return (onsite[None, :, :, None] * middle - neighbours) / HOP_SCALE


def rotate(picked):
    return jnp.stack([-picked[1], picked[0]])


def combine_pairs(products):
    return jnp.stack([products[0, 0] + products[1, 1], products[1, 0] - products[0, 1]])


def shards(occupied, disorder, region_cols, cheb_coef, prior_corr):
    band_rows = occupied.shape[1]
    term_count = cheb_coef.shape[1]
    current = occupied.astype(jnp.float32)

    def contribution(state, degree):
        picked = jnp.take(state, region_cols, axis=2)
        return cheb_coef[0, degree] * picked + cheb_coef[1, degree] * rotate(picked)

    summed = contribution(current, 0)
    previous = current
    onsite = disorder.astype(jnp.float32) * LEVEL_STEP
    for degree in range(1, term_count):
        padded = padded_2(current, (("rows", 1),), 1)
        applied = apply_rows(padded, onsite)
        following = applied if degree == 1 else 2.0 * applied - previous
        previous, current = (current, following)
        summed = summed + contribution(current, degree)
    tile_rows = band_rows * region_cols.shape[0]
    evolved = summed.astype(jnp.bfloat16).reshape(2, tile_rows, summed.shape[3])
    row_panel = lax.all_gather(evolved, "orb", axis=2, tiled=True)
    column_all = lax.all_gather(evolved, "rows", axis=1, tiled=True)
    column_panel = lax.all_to_all(column_all, "orb", split_axis=1, concat_axis=2, tiled=True)
    products = jnp.einsum(
        "cim,djm->cdij", row_panel, column_panel, preferred_element_type=jnp.float32
    )
    tile_sum = combine_pairs(products)
    return prior_corr.astype(jnp.float32) + tile_sum


LANES = 128
FRAME = 16
MESH = pl.DeviceIdType.MESH


def quench_kernel(
    row_count, occupied, disorder, region_cols, cheb_coef, out,
    fields, turned, levels, hot, window, picks, operator, product, kept, leaving,
    nearby, crossed, outgoing, incoming, columns, weights,
    here, load_sem, level_send, level_recv, field_send, field_recv,
    near_send, near_recv, cross_send, cross_recv, block_send, block_recv,
):
    r = lax.axis_index("rows")
    o = lax.axis_index("orb")
    g = o % 2
    x = o // 2
    band, width = disorder.shape
    height = band * row_count
    terms = cheb_coef.shape[1]
    reach = terms - 1
    acols = region_cols.shape[0]
    tile = out.shape[1]
    chips = 2 * row_count
    mine = 2 * r + x
    half = row_count // 2
    side = r // half
    place = r % half
    pair = r + 1 - 2 * place
    across = (r + half) % row_count
    owner = g == side
    passer = jnp.logical_not(owner)
    spots = 2 * LANES

    def remote(src, dst, send, recv, row, orb):
        return pltpu.make_async_remote_copy(
            src_ref=src, dst_ref=dst, send_sem=send, recv_sem=recv,
            device_id={"rows": row, "orb": orb}, device_id_type=MESH,
        )

    barrier = pltpu.get_barrier_semaphore()

    def greet(row, orb):
        pl.semaphore_signal(
            barrier, inc=1, device_id={"rows": row, "orb": orb}, device_id_type=MESH
        )

    for k in range(1, 4):
        greet(r, (o + k) % 4)
    for k in range(1, row_count):
        pl.when(r + k < row_count)(lambda k=k: greet((r + k) % row_count, o))

    def chunk(i, which):
        return occupied.at[:, i, :, pl.ds(pl.multiple_of(which * LANES, LANES), LANES)]

    loads = [
        pltpu.make_async_copy(disorder, levels.at[r], load_sem.at[0]),
        pltpu.make_async_copy(region_cols, columns, load_sem.at[1]),
        pltpu.make_async_copy(cheb_coef, weights, load_sem.at[2]),
    ]
    for load in loads:
        load.start()
    def own_load(slot, i):
        return pltpu.make_async_copy(
            chunk(i, place if slot == 0 else 1 - place), fields.at[slot, i], field_recv.at[slot, i]
        )

    for i in range(band):
        own_load(0, i).start()

    @pl.when(owner)
    def _():
        for i in range(band):
            own_load(1, i).start()

    for load in loads:
        load.wait()

    pl.semaphore_wait(barrier, 3 + r)

    def level_copy(slot, kind, row):
        return remote(
            levels.at[slot], levels.at[slot], level_send.at[kind], level_recv.at[slot], row, o
        )

    def down(k):
        return level_copy(r, k - 1, (r + row_count - k) % row_count)

    def up(k):
        return level_copy(r, row_count + k - 2, (r + k) % row_count)

    def field_copy(i):
        return remote(
            chunk(i, 1 - place), fields.at[1, i], field_send.at[i],
            field_recv.at[1, i], pair, o,
        )

    def answer(k):
        pl.semaphore_signal(
            here.at[r], inc=1,
            device_id={"rows": (r + row_count - k) % row_count, "orb": o}, device_id_type=MESH,
        )

    def send_fields():
        for i in range(band):
            field_copy(i).start()

    def climb(k):
        pl.semaphore_wait(here.at[(r + k) % row_count], 1)
        up(k).start()

    for k in range(1, row_count):
        pl.when(r >= k)(functools.partial(answer, k))
    for k in range(row_count - 1, 0, -1):
        pl.when(r >= k)(lambda k=k: down(k).start())
    pl.when(passer & (place == 1))(send_fields)
    pl.when(r + 1 < row_count)(functools.partial(climb, 1))
    pl.when(passer & (place == 0))(send_fields)

    lane = lax.broadcasted_iota(jnp.int32, (1, LANES), 1)
    cols = jnp.zeros((1, LANES), jnp.int32)
    for a in range(acols):
        cols = jnp.where(lane % acols == a, columns[a], cols)
    offset = lax.broadcasted_iota(jnp.int32, (width, LANES), 0) - cols + reach
    offset = jnp.where(offset < 0, offset + width, offset)
    offset = jnp.where(offset >= width, offset - width, offset)
    for d in range(1, 2 * reach):
        hot[d - 1] = jnp.where(offset == d, 1.0, 0.0).astype(jnp.bfloat16)

    first = cols - reach
    first = jnp.where(first < 0, first + width, first)
    first = jnp.concatenate([first, first], axis=1)
    slide = jnp.broadcast_to(first % FRAME, (2 * FRAME, spots))
    strip = jnp.broadcast_to(first // FRAME, (FRAME, spots))
    strips = width // FRAME
    for j in range(strips):
        picks[j] = jnp.where(strip == j, 1.0, 0.0).astype(jnp.bfloat16)

    def turn(slot, i):
        k = band * slot + i
        for part in range(2):
            turned[part * LANES : (part + 1) * LANES, k * width : (k + 1) * width] = (
                fields[slot, i, part].T
            )

    for i in range(band):
        own_load(0, i).wait()
        turn(0, i)

    @pl.when(owner)
    def _():
        for i in range(band):
            own_load(1, i).wait()
            turn(1, i)

    for k in range(2, row_count):
        pl.when(r + k < row_count)(functools.partial(climb, k))
    for k in range(1, row_count):
        slot = (r + k) % row_count
        level_copy(slot, 0, (r + 1) % row_count).wait_recv()

    onsite = jnp.concatenate([levels[k] for k in range(row_count)], axis=0)
    onsite = (onsite.astype(jnp.float32) * LEVEL_STEP).astype(jnp.bfloat16)

    local_levels = {}
    for d in range(1, 2 * reach):
        here = jnp.dot(onsite, hot[d - 1], preferred_element_type=jnp.float32)
        local_levels[d] = jnp.concatenate([here, here], axis=1)

    lane = lax.broadcasted_iota(jnp.int32, (height, spots), 1)
    row_id = lax.broadcasted_iota(jnp.int32, (height, spots), 0)
    start = jnp.where(row_id == lane // acols, 1.0, 0.0)
    previous, current = {}, {reach: start}
    real = {reach: weights[0, 0] * start}
    imag = {reach: weights[1, 0] * start}
    for degree in range(1, terms):
        following = {}
        for d in range(reach - degree, reach + degree + 1):
            total = None
            if d in current:
                here = current[d]
                total = local_levels[d] * here - (
                    pltpu.roll(here, 1, 0) + pltpu.roll(here, height - 1, 0)
                )
            for beside in (d - 1, d + 1):
                if beside in current:
                    there = current[beside]
                    total = -there if total is None else total - there
            value = total * ((1.0 if degree == 1 else 2.0) / HOP_SCALE)
            if d in previous:
                value = value - previous[d]
            following[d] = value
            more_real = weights[0, degree] * value
            more_imag = weights[1, degree] * value
            real[d] = real[d] + more_real if d in real else more_real
            imag[d] = imag[d] + more_imag if d in imag else more_imag
        previous, current = current, following
    for part, parts in ((0, real), (1, imag)):
        for d in range(FRAME):
            rows = pl.ds((part * FRAME + d) * height, height)
            value = parts[d] if d in parts else jnp.zeros((height, spots), jnp.float32)
            window[0, rows, :] = value[:, :LANES]
            window[1, rows, :] = value[:, LANES:]

    def expand(slot, i):
        k = band * slot + i
        where = place if slot == 0 else 1 - place
        y = band * (half * side + where) + i
        for part in range(2):
            rows = pl.ds(part * FRAME * height + y, FRAME, stride=height)
            bare = jnp.concatenate([window[0, rows, :], window[1, rows, :]], axis=1)
            frame = jnp.concatenate([bare, jnp.zeros_like(bare)], axis=0)
            step = 1
            while step < FRAME:
                moved = pltpu.roll(frame, step, 0)
                frame = jnp.where((slide & step) != 0, moved, frame)
                step *= 2
            high = frame.astype(jnp.bfloat16)
            low = (frame - high.astype(jnp.float32)).astype(jnp.bfloat16)
            for kind, value in ((0, high), (1, low)):
                upper, lower = value[:FRAME], value[FRAME:]
                for j in range(strips):
                    operator[
                        kind, k * width + j * FRAME : k * width + (j + 1) * FRAME,
                        part * spots : (part + 1) * spots,
                    ] = upper * picks[j] + lower * picks[(j - 1) % strips]

    def applied(slot, at):
        rows = slice(slot * band * width, (slot + 1) * band * width)
        ats = slice(at * band * width, (at + 1) * band * width)
        total = jnp.dot(
            turned[:, rows], operator[0, ats, :], preferred_element_type=jnp.float32
        ) + jnp.dot(turned[:, rows], operator[1, ats, :], preferred_element_type=jnp.float32)
        return total

    def pieces(total):
        return (
            total[:LANES, :spots] - total[LANES:, spots:],
            total[LANES:, :spots] + total[:LANES, spots:],
        )

    def near_copy():
        return remote(leaving, nearby, near_send, near_recv, pair, o)

    def cross_copy():
        return remote(leaving, crossed, cross_send, cross_recv, across, o)

    def block_copy(chip, part, slot):
        return remote(
            outgoing.at[2 * chip + part], incoming.at[slot], block_send.at[2 * chip + part],
            block_recv.at[slot], chip // 2, 2 * (chip % 2) + part,
        )

    for i in range(band):
        expand(0, i)

    @pl.when(passer)
    def _():
        product[...] = applied(0, 0)
        for i in range(band):
            expand(1, i)
        for i in range(band):
            field_copy(i).wait_recv()
            turn(1, i)
        parts = pieces(product[...] + applied(1, 1))
        leaving[0] = parts[0].astype(jnp.bfloat16)
        leaving[1] = parts[1].astype(jnp.bfloat16)
        cross_copy().start()

    @pl.when(owner)
    def _():
        parts = pieces(applied(1, 0))
        leaving[0] = parts[0].astype(jnp.bfloat16)
        leaving[1] = parts[1].astype(jnp.bfloat16)
        near_copy().start()
        parts = pieces(applied(0, 0))
        kept[0] = parts[0]
        kept[1] = parts[1]
        near_copy().wait_recv()
        cross_copy().wait_recv()
        evolved = [
            (kept[part] + nearby[part].astype(jnp.float32) + crossed[part].astype(jnp.float32))
            .astype(jnp.bfloat16)
            .T
            for part in range(2)
        ]
        left = jnp.concatenate([evolved[0], evolved[1]], axis=1)
        flipped = jnp.concatenate([-evolved[1], evolved[0]], axis=1)
        rights = []
        for column in range(4):
            rows = slice(column * tile, (column + 1) * tile)
            rights.append(left[rows])
            rights.append(flipped[rows])
        blocks = lax.dot_general(
            left, jnp.concatenate(rights, axis=0), (((1,), (1,)), ((), ())),
            preferred_element_type=jnp.float32,
        ).astype(jnp.bfloat16)
        for row in range(row_count):
            for column in range(4):
                outgoing[4 * row + column] = blocks[
                    row * tile : (row + 1) * tile, column * LANES : (column + 1) * LANES
                ]
        for chip in range(chips):
            for part in range(2):

                @pl.when((mine != chip) | (g != part))
                def _():
                    block_copy(chip, part, mine).start()

        incoming[mine] = outgoing[2 * mine + g]

    pl.when(passer)(lambda: block_copy(0, 0, mine).wait_recv())
    total = incoming[mine].astype(jnp.float32)
    for k in range(1, chips):
        slot = (mine + chips - k) % chips
        block_copy(0, 0, slot).wait_recv()
        total = total + incoming[slot].astype(jnp.float32)
    out[0] = total[:, :tile]
    out[1] = total[:, tile:]

    for k in range(1, row_count):
        pl.when(r >= k)(lambda k=k: down(k).wait_send())
        pl.when(r + k < row_count)(lambda k=k: up(k).wait_send())

    @pl.when(passer)
    def _():
        for i in range(band):
            field_copy(i).wait_send()
        cross_copy().wait_send()

    @pl.when(owner)
    def _():
        near_copy().wait_send()
        for chip in range(chips):
            for part in range(2):

                @pl.when((mine != chip) | (g != part))
                def _():
                    block_copy(chip, part, mine).wait_send()


def fused_step(row_count, occupied, disorder, region_cols, cheb_coef, prior_corr):
    band, width = disorder.shape
    terms = cheb_coef.shape[1]
    tile = prior_corr.shape[1]
    height = band * row_count
    chips = 2 * row_count
    half = row_count // 2
    spots = 2 * LANES
    dma = pltpu.SemaphoreType.DMA
    anywhere = pl.BlockSpec(memory_space=pl.ANY)
    corr = pl.pallas_call(
        functools.partial(quench_kernel, row_count),
        out_shape=pltpu.VMEM(prior_corr.shape, jnp.float32),
        in_specs=[anywhere] * 4,
        out_specs=pl.BlockSpec(memory_space=pltpu.VMEM),
        scratch_shapes=[
            pltpu.VMEM((2, band, 2, width, LANES), jnp.bfloat16),
            pltpu.VMEM((2 * LANES, height // 2 * width), jnp.bfloat16),
            pltpu.VMEM((row_count, band, width), jnp.int32),
            pltpu.VMEM((2 * terms - 3, width, LANES), jnp.bfloat16),
            pltpu.VMEM((2, 2 * FRAME * height, LANES), jnp.float32),
            pltpu.VMEM((width // FRAME, FRAME, spots), jnp.bfloat16),
            pltpu.VMEM((2, height // 2 * width, 2 * spots), jnp.bfloat16),
            pltpu.VMEM((2 * LANES, 2 * spots), jnp.float32),
            pltpu.VMEM((2, LANES, spots), jnp.float32),
            pltpu.VMEM((2, LANES, spots), jnp.bfloat16),
            pltpu.VMEM((2, LANES, spots), jnp.bfloat16),
            pltpu.VMEM((2, LANES, spots), jnp.bfloat16),
            pltpu.VMEM((2 * chips, tile, LANES), jnp.bfloat16),
            pltpu.VMEM((chips, tile, LANES), jnp.bfloat16),
            pltpu.SMEM(region_cols.shape, jnp.int32),
            pltpu.SMEM(cheb_coef.shape, jnp.float32),
            pltpu.SemaphoreType.REGULAR((row_count,)),
            dma((3,)),
            dma((2 * row_count - 2,)),
            dma((row_count,)),
            dma((band,)),
            dma((2, band)),
            dma,
            dma,
            dma,
            dma,
            dma((2 * chips,)),
            dma((chips,)),
        ],
        compiler_params=pltpu.CompilerParams(collective_id=0, has_side_effects=True),
    )(occupied, disorder, region_cols, cheb_coef)
    return prior_corr.astype(jnp.float32) + corr


def local_step(row_count, orb_count, occupied, disorder, region_cols, cheb_coef, prior_corr):
    band, width, orbitals = occupied.shape[1:]
    terms = cheb_coef.shape[1]
    height = band * row_count
    sites = height * region_cols.shape[0]
    fused = (
        orb_count == 4
        and row_count == 4
        and sites == 2 * LANES
        and 2 * orbitals == row_count * LANES
        and orbitals == 2 * LANES
        and height % 8 == 0
        and width % LANES == 0
        and width >= 2 * FRAME
        and 2 * terms <= FRAME
        and LANES % region_cols.shape[0] == 0
        and prior_corr.shape[1:] == (LANES // 2, LANES // 2)
    )
    if fused:
        return fused_step(row_count, occupied, disorder, region_cols, cheb_coef, prior_corr)
    return shards(occupied, disorder, region_cols, cheb_coef, prior_corr)


def solution(mesh):
    return jax.shard_map(
        functools.partial(local_step, mesh.shape["rows"], mesh.shape["orb"]),
        mesh=mesh,
        in_specs=(
            P(None, ("real", "rows"), None, "orb"),
            P(("real", "rows"), None),
            P(),
            P(),
            P(None, ("real", "rows"), "orb"),
        ),
        out_specs=P(None, ("real", "rows"), "orb"),
        check_vma=False,
    )
```

```python
import functools

import jax
import jax.numpy as jnp
from jax import lax
from jax.experimental import pallas as pl
from jax.experimental.pallas import tpu as pltpu
from jax.sharding import PartitionSpec as P

HOP_SCALE = 5.25
LEVEL_STEP = 0.125


def padded_2(cells, sides, width):
    for axis, dim in sides:
        count = lax.axis_size(axis)
        head = lax.slice_in_dim(cells, 0, width, axis=dim)
        tail = lax.slice_in_dim(cells, cells.shape[dim] - width, cells.shape[dim], axis=dim)
        cells = jnp.concatenate(
            [
                lax.ppermute(tail, axis, [(i, (i + 1) % count) for i in range(count)]),
                cells,
                lax.ppermute(head, axis, [((i + 1) % count, i) for i in range(count)]),
            ],
            axis=dim,
        )
    return cells


def apply_rows(padded, onsite):
    middle = padded[:, 1:-1]
    neighbours = padded[:, 2:] + padded[:, :-2] + jnp.roll(middle, -1, 2) + jnp.roll(middle, 1, 2)
    return (onsite[None, :, :, None] * middle - neighbours) / HOP_SCALE


def rotate(picked):
    return jnp.stack([-picked[1], picked[0]])


def combine_pairs(products):
    return jnp.stack([products[0, 0] + products[1, 1], products[1, 0] - products[0, 1]])


def shards(occupied, disorder, region_cols, cheb_coef, prior_corr):
    band_rows = occupied.shape[1]
    term_count = cheb_coef.shape[1]
    current = occupied.astype(jnp.float32)

    def contribution(state, degree):
        picked = jnp.take(state, region_cols, axis=2)
        return cheb_coef[0, degree] * picked + cheb_coef[1, degree] * rotate(picked)

    summed = contribution(current, 0)
    previous = current
    onsite = disorder.astype(jnp.float32) * LEVEL_STEP
    for degree in range(1, term_count):
        padded = padded_2(current, (("rows", 1),), 1)
        applied = apply_rows(padded, onsite)
        following = applied if degree == 1 else 2.0 * applied - previous
        previous, current = (current, following)
        summed = summed + contribution(current, degree)
    tile_rows = band_rows * region_cols.shape[0]
    evolved = summed.astype(jnp.bfloat16).reshape(2, tile_rows, summed.shape[3])
    row_panel = lax.all_gather(evolved, "orb", axis=2, tiled=True)
    column_all = lax.all_gather(evolved, "rows", axis=1, tiled=True)
    column_panel = lax.all_to_all(column_all, "orb", split_axis=1, concat_axis=2, tiled=True)
    products = jnp.einsum(
        "cim,djm->cdij", row_panel, column_panel, preferred_element_type=jnp.float32
    )
    tile_sum = combine_pairs(products)
    return prior_corr.astype(jnp.float32) + tile_sum


LANES = 128
FRAME = 16
MESH = pl.DeviceIdType.MESH


def quench_kernel(
    row_count, occupied, disorder, region_cols, cheb_coef, out,
    fields, turned, levels, hot, window, picks, operator, product, kept, leaving,
    nearby, crossed, outgoing, incoming, columns, weights,
    here, load_sem, level_send, level_recv, field_send, field_recv,
    near_send, near_recv, cross_send, cross_recv, block_send, block_recv,
):
    r = lax.axis_index("rows")
    o = lax.axis_index("orb")
    g = o % 2
    x = o // 2
    band, width = disorder.shape
    height = band * row_count
    terms = cheb_coef.shape[1]
    reach = terms - 1
    acols = region_cols.shape[0]
    tile = out.shape[1]
    chips = 2 * row_count
    mine = 2 * r + x
    half = row_count // 2
    side = r // half
    place = r % half
    pair = r + 1 - 2 * place
    across = (r + half) % row_count
    owner = g == side
    passer = jnp.logical_not(owner)
    spots = 2 * LANES

    def remote(src, dst, send, recv, row, orb):
        return pltpu.make_async_remote_copy(
            src_ref=src, dst_ref=dst, send_sem=send, recv_sem=recv,
            device_id={"rows": row, "orb": orb}, device_id_type=MESH,
        )

    barrier = pltpu.get_barrier_semaphore()

    def greet(row, orb):
        pl.semaphore_signal(
            barrier, inc=1, device_id={"rows": row, "orb": orb}, device_id_type=MESH
        )

    for k in range(1, 4):
        greet(r, (o + k) % 4)
    for k in range(1, row_count):
        pl.when(r + k < row_count)(lambda k=k: greet((r + k) % row_count, o))

    def chunk(i, which):
        return occupied.at[:, i, :, pl.ds(pl.multiple_of(which * LANES, LANES), LANES)]

    loads = [
        pltpu.make_async_copy(disorder, levels.at[r], load_sem.at[0]),
        pltpu.make_async_copy(region_cols, columns, load_sem.at[1]),
        pltpu.make_async_copy(cheb_coef, weights, load_sem.at[2]),
    ]
    for load in loads:
        load.start()
    def own_load(slot, i):
        return pltpu.make_async_copy(
            chunk(i, place if slot == 0 else 1 - place), fields.at[slot, i], field_recv.at[slot, i]
        )

    for i in range(band):
        own_load(0, i).start()

    @pl.when(owner)
    def _():
        for i in range(band):
            own_load(1, i).start()

    pl.semaphore_wait(barrier, 3 + r)

    def level_copy(slot, kind, row):
        return remote(
            disorder, levels.at[slot], level_send.at[kind], level_recv.at[slot], row, o
        )

    def down(k):
        return level_copy(r, k - 1, (r + row_count - k) % row_count)

    def up(k):
        return level_copy(r, row_count + k - 2, (r + k) % row_count)

    def field_copy(i):
        return remote(
            chunk(i, 1 - place), fields.at[1, i], field_send.at[i],
            field_recv.at[1, i], pair, o,
        )

    def answer(k):
        pl.semaphore_signal(
            here.at[r], inc=1,
            device_id={"rows": (r + row_count - k) % row_count, "orb": o}, device_id_type=MESH,
        )

    def send_fields():
        for i in range(band):
            field_copy(i).start()

    def climb(k):
        pl.semaphore_wait(here.at[(r + k) % row_count], 1)
        up(k).start()

    for k in range(1, row_count):
        pl.when(r >= k)(functools.partial(answer, k))
    for k in range(row_count - 1, 0, -1):
        pl.when(r >= k)(lambda k=k: down(k).start())
    pl.when(passer & (place == 1))(send_fields)
    pl.when(r + 1 < row_count)(functools.partial(climb, 1))
    pl.when(passer & (place == 0))(send_fields)
    for load in loads:
        load.wait()

    lane = lax.broadcasted_iota(jnp.int32, (1, LANES), 1)
    cols = jnp.zeros((1, LANES), jnp.int32)
    for a in range(acols):
        cols = jnp.where(lane % acols == a, columns[a], cols)
    offset = lax.broadcasted_iota(jnp.int32, (width, LANES), 0) - cols + reach
    offset = jnp.where(offset < 0, offset + width, offset)
    offset = jnp.where(offset >= width, offset - width, offset)
    for d in range(1, 2 * reach):
        hot[d - 1] = jnp.where(offset == d, 1.0, 0.0).astype(jnp.bfloat16)

    first = cols - reach
    first = jnp.where(first < 0, first + width, first)
    first = jnp.concatenate([first, first], axis=1)
    slide = jnp.broadcast_to(first % FRAME, (2 * FRAME, spots))
    strip = jnp.broadcast_to(first // FRAME, (FRAME, spots))
    strips = width // FRAME
    for j in range(strips):
        picks[j] = jnp.where(strip == j, 1.0, 0.0).astype(jnp.bfloat16)

    def turn(slot, i):
        k = band * slot + i
        for part in range(2):
            turned[part * LANES : (part + 1) * LANES, k * width : (k + 1) * width] = (
                fields[slot, i, part].T
            )

    for i in range(band):
        own_load(0, i).wait()
        turn(0, i)

    @pl.when(owner)
    def _():
        for i in range(band):
            own_load(1, i).wait()
            turn(1, i)

    for k in range(2, row_count):
        pl.when(r + k < row_count)(functools.partial(climb, k))
    for k in range(1, row_count):
        slot = (r + k) % row_count
        level_copy(slot, 0, (r + 1) % row_count).wait_recv()

    onsite = jnp.concatenate([levels[k] for k in range(row_count)], axis=0)
    onsite = (onsite.astype(jnp.float32) * LEVEL_STEP).astype(jnp.bfloat16)

    local_levels = {}
    for d in range(1, 2 * reach):
        here = jnp.dot(onsite, hot[d - 1], preferred_element_type=jnp.float32)
        local_levels[d] = jnp.concatenate([here, here], axis=1)

    lane = lax.broadcasted_iota(jnp.int32, (height, spots), 1)
    row_id = lax.broadcasted_iota(jnp.int32, (height, spots), 0)
    start = jnp.where(row_id == lane // acols, 1.0, 0.0)
    previous, current = {}, {reach: start}
    real = {reach: weights[0, 0] * start}
    imag = {reach: weights[1, 0] * start}
    for degree in range(1, terms):
        following = {}
        for d in range(reach - degree, reach + degree + 1):
            total = None
            if d in current:
                here = current[d]
                total = local_levels[d] * here - (
                    pltpu.roll(here, 1, 0) + pltpu.roll(here, height - 1, 0)
                )
            for beside in (d - 1, d + 1):
                if beside in current:
                    there = current[beside]
                    total = -there if total is None else total - there
            value = total * ((1.0 if degree == 1 else 2.0) / HOP_SCALE)
            if d in previous:
                value = value - previous[d]
            following[d] = value
            more_real = weights[0, degree] * value
            more_imag = weights[1, degree] * value
            real[d] = real[d] + more_real if d in real else more_real
            imag[d] = imag[d] + more_imag if d in imag else more_imag
        previous, current = current, following
    for part, parts in ((0, real), (1, imag)):
        for d in range(FRAME):
            rows = pl.ds((part * FRAME + d) * height, height)
            value = parts[d] if d in parts else jnp.zeros((height, spots), jnp.float32)
            window[0, rows, :] = value[:, :LANES]
            window[1, rows, :] = value[:, LANES:]

    def expand(slot, i):
        k = band * slot + i
        where = place if slot == 0 else 1 - place
        y = band * (half * side + where) + i
        for part in range(2):
            rows = pl.ds(part * FRAME * height + y, FRAME, stride=height)
            bare = jnp.concatenate([window[0, rows, :], window[1, rows, :]], axis=1)
            frame = jnp.concatenate([bare, jnp.zeros_like(bare)], axis=0)
            step = 1
            while step < FRAME:
                moved = pltpu.roll(frame, step, 0)
                frame = jnp.where((slide & step) != 0, moved, frame)
                step *= 2
            high = frame.astype(jnp.bfloat16)
            low = (frame - high.astype(jnp.float32)).astype(jnp.bfloat16)
            for kind, value in ((0, high), (1, low)):
                upper, lower = value[:FRAME], value[FRAME:]
                for j in range(strips):
                    strip = upper * picks[j] + lower * picks[(j - 1) % strips]
                    rows = slice(k * width + j * FRAME, k * width + (j + 1) * FRAME)
                    for s in range(2):
                        operator[kind, s, rows, part * LANES : (part + 1) * LANES] = strip[
                            :, s * LANES : (s + 1) * LANES
                        ]

    def applied(slot, at, s):
        rows = slice(slot * band * width, (slot + 1) * band * width)
        ats = slice(at * band * width, (at + 1) * band * width)
        return jnp.dot(
            turned[:, rows], operator[0, s, ats, :], preferred_element_type=jnp.float32
        ) + jnp.dot(turned[:, rows], operator[1, s, ats, :], preferred_element_type=jnp.float32)

    def pieces(total):
        return (
            total[:LANES, :LANES] - total[LANES:, LANES:],
            total[LANES:, :LANES] + total[:LANES, LANES:],
        )

    def near_copy(s):
        return remote(
            leaving.at[s], nearby.at[s], near_send.at[s], near_recv.at[s], pair, o
        )

    def cross_copy(s):
        return remote(
            leaving.at[s], crossed.at[s], cross_send.at[s], cross_recv.at[s], across, o
        )

    def leave(s, total, copy):
        parts = pieces(total)
        for part in range(2):
            leaving[s, part] = parts[part].astype(jnp.bfloat16)
        copy(s).start()

    def block_copy(chip, part, slot):
        return remote(
            outgoing.at[2 * chip + part], incoming.at[slot], block_send.at[2 * chip + part],
            block_recv.at[slot], chip // 2, 2 * (chip % 2) + part,
        )

    for i in range(band):
        expand(0, i)

    @pl.when(passer)
    def _():
        for s in range(2):
            product[s] = applied(0, 0, s)
        for i in range(band):
            expand(1, i)
        for i in range(band):
            field_copy(i).wait_recv()
            turn(1, i)
        for s in range(2):
            leave(s, product[s] + applied(1, 1, s), cross_copy)

    @pl.when(owner)
    def _():
        for s in range(2):
            parts = pieces(applied(0, 0, s))
            kept[s, 0] = parts[0]
            kept[s, 1] = parts[1]
        for s in range(2):
            leave(s, applied(1, 0, s), near_copy)
        for s in range(2):
            near_copy(s).wait_recv()
            kept[s] = kept[s] + nearby[s].astype(jnp.float32)
        lefts, turns = [], []
        for s in range(2):
            cross_copy(s).wait_recv()
            whole = (kept[s] + crossed[s].astype(jnp.float32)).astype(jnp.bfloat16)
            real_part, imag_part = whole[0].T, whole[1].T
            lefts.append(jnp.concatenate([real_part, imag_part], axis=1))
            turns.append(jnp.concatenate([-imag_part, real_part], axis=1))
        left = jnp.concatenate(lefts, axis=0)
        flipped = jnp.concatenate(turns, axis=0)
        rights = []
        for column in range(4):
            rows = slice(column * tile, (column + 1) * tile)
            rights.append(left[rows])
            rights.append(flipped[rows])
        right = jnp.concatenate(rights, axis=0)
        for row in (0, *range(row_count - 1, 0, -1)):
            blocks = lax.dot_general(
                left[row * tile : (row + 1) * tile], right, (((1,), (1,)), ((), ())),
                preferred_element_type=jnp.float32,
            ).astype(jnp.bfloat16)
            for column in range(4):
                outgoing[4 * row + column] = blocks[:, column * LANES : (column + 1) * LANES]
            for column in range(4):
                chip, part = 2 * row + column // 2, column % 2

                @pl.when((mine != chip) | (g != part))
                def _():
                    block_copy(chip, part, mine).start()

        incoming[mine] = outgoing[2 * mine + g]

    pl.when(passer)(lambda: block_copy(0, 0, mine).wait_recv())
    total = incoming[mine].astype(jnp.float32)
    for k in range(1, chips):
        slot = (mine + chips - k) % chips
        block_copy(0, 0, slot).wait_recv()
        total = total + incoming[slot].astype(jnp.float32)
    out[0] = total[:, :tile]
    out[1] = total[:, tile:]

    for k in range(1, row_count):
        pl.when(r >= k)(lambda k=k: down(k).wait_send())
        pl.when(r + k < row_count)(lambda k=k: up(k).wait_send())

    @pl.when(passer)
    def _():
        for i in range(band):
            field_copy(i).wait_send()
        for s in range(2):
            cross_copy(s).wait_send()

    @pl.when(owner)
    def _():
        for s in range(2):
            near_copy(s).wait_send()
        for chip in range(chips):
            for part in range(2):

                @pl.when((mine != chip) | (g != part))
                def _():
                    block_copy(chip, part, mine).wait_send()


def fused_step(row_count, occupied, disorder, region_cols, cheb_coef, prior_corr):
    band, width = disorder.shape
    terms = cheb_coef.shape[1]
    tile = prior_corr.shape[1]
    height = band * row_count
    chips = 2 * row_count
    half = row_count // 2
    spots = 2 * LANES
    dma = pltpu.SemaphoreType.DMA
    anywhere = pl.BlockSpec(memory_space=pl.ANY)
    corr = pl.pallas_call(
        functools.partial(quench_kernel, row_count),
        out_shape=pltpu.VMEM(prior_corr.shape, jnp.float32),
        in_specs=[anywhere] * 4,
        out_specs=pl.BlockSpec(memory_space=pltpu.VMEM),
        scratch_shapes=[
            pltpu.VMEM((2, band, 2, width, LANES), jnp.bfloat16),
            pltpu.VMEM((2 * LANES, height // 2 * width), jnp.bfloat16),
            pltpu.VMEM((row_count, band, width), jnp.int32),
            pltpu.VMEM((2 * terms - 3, width, LANES), jnp.bfloat16),
            pltpu.VMEM((2, 2 * FRAME * height, LANES), jnp.float32),
            pltpu.VMEM((width // FRAME, FRAME, spots), jnp.bfloat16),
            pltpu.VMEM((2, 2, height // 2 * width, spots), jnp.bfloat16),
            pltpu.VMEM((2, 2 * LANES, spots), jnp.float32),
            pltpu.VMEM((2, 2, LANES, LANES), jnp.float32),
            pltpu.VMEM((2, 2, LANES, LANES), jnp.bfloat16),
            pltpu.VMEM((2, 2, LANES, LANES), jnp.bfloat16),
            pltpu.VMEM((2, 2, LANES, LANES), jnp.bfloat16),
            pltpu.VMEM((2 * chips, tile, LANES), jnp.bfloat16),
            pltpu.VMEM((chips, tile, LANES), jnp.bfloat16),
            pltpu.SMEM(region_cols.shape, jnp.int32),
            pltpu.SMEM(cheb_coef.shape, jnp.float32),
            pltpu.SemaphoreType.REGULAR((row_count,)),
            dma((3,)),
            dma((2 * row_count - 2,)),
            dma((row_count,)),
            dma((band,)),
            dma((2, band)),
            dma((2,)),
            dma((2,)),
            dma((2,)),
            dma((2,)),
            dma((2 * chips,)),
            dma((chips,)),
        ],
        compiler_params=pltpu.CompilerParams(collective_id=0, has_side_effects=True),
    )(occupied, disorder, region_cols, cheb_coef)
    return prior_corr.astype(jnp.float32) + corr


def local_step(row_count, orb_count, occupied, disorder, region_cols, cheb_coef, prior_corr):
    band, width, orbitals = occupied.shape[1:]
    terms = cheb_coef.shape[1]
    height = band * row_count
    sites = height * region_cols.shape[0]
    fused = (
        orb_count == 4
        and row_count == 4
        and sites == 2 * LANES
        and 2 * orbitals == row_count * LANES
        and orbitals == 2 * LANES
        and height % 8 == 0
        and width % LANES == 0
        and width >= 2 * FRAME
        and 2 * terms <= FRAME
        and LANES % region_cols.shape[0] == 0
        and prior_corr.shape[1:] == (LANES // 2, LANES // 2)
    )
    if fused:
        return fused_step(row_count, occupied, disorder, region_cols, cheb_coef, prior_corr)
    return shards(occupied, disorder, region_cols, cheb_coef, prior_corr)


def solution(mesh):
    return jax.shard_map(
        functools.partial(local_step, mesh.shape["rows"], mesh.shape["orb"]),
        mesh=mesh,
        in_specs=(
            P(None, ("real", "rows"), None, "orb"),
            P(("real", "rows"), None),
            P(),
            P(),
            P(None, ("real", "rows"), "orb"),
        ),
        out_specs=P(None, ("real", "rows"), "orb"),
        check_vma=False,
    )
```

```python
import functools

import jax
import jax.numpy as jnp
from jax import lax
from jax.experimental import pallas as pl
from jax.experimental.pallas import tpu as pltpu
from jax.sharding import PartitionSpec as P

HOP_SCALE = 5.25
LEVEL_STEP = 0.125


def padded_2(cells, sides, width):
    for axis, dim in sides:
        count = lax.axis_size(axis)
        head = lax.slice_in_dim(cells, 0, width, axis=dim)
        tail = lax.slice_in_dim(cells, cells.shape[dim] - width, cells.shape[dim], axis=dim)
        cells = jnp.concatenate(
            [
                lax.ppermute(tail, axis, [(i, (i + 1) % count) for i in range(count)]),
                cells,
                lax.ppermute(head, axis, [((i + 1) % count, i) for i in range(count)]),
            ],
            axis=dim,
        )
    return cells


def apply_rows(padded, onsite):
    middle = padded[:, 1:-1]
    neighbours = padded[:, 2:] + padded[:, :-2] + jnp.roll(middle, -1, 2) + jnp.roll(middle, 1, 2)
    return (onsite[None, :, :, None] * middle - neighbours) / HOP_SCALE


def rotate(picked):
    return jnp.stack([-picked[1], picked[0]])


def combine_pairs(products):
    return jnp.stack([products[0, 0] + products[1, 1], products[1, 0] - products[0, 1]])


def shards(occupied, disorder, region_cols, cheb_coef, prior_corr):
    band_rows = occupied.shape[1]
    term_count = cheb_coef.shape[1]
    current = occupied.astype(jnp.float32)

    def contribution(state, degree):
        picked = jnp.take(state, region_cols, axis=2)
        return cheb_coef[0, degree] * picked + cheb_coef[1, degree] * rotate(picked)

    summed = contribution(current, 0)
    previous = current
    onsite = disorder.astype(jnp.float32) * LEVEL_STEP
    for degree in range(1, term_count):
        padded = padded_2(current, (("rows", 1),), 1)
        applied = apply_rows(padded, onsite)
        following = applied if degree == 1 else 2.0 * applied - previous
        previous, current = (current, following)
        summed = summed + contribution(current, degree)
    tile_rows = band_rows * region_cols.shape[0]
    evolved = summed.astype(jnp.bfloat16).reshape(2, tile_rows, summed.shape[3])
    row_panel = lax.all_gather(evolved, "orb", axis=2, tiled=True)
    column_all = lax.all_gather(evolved, "rows", axis=1, tiled=True)
    column_panel = lax.all_to_all(column_all, "orb", split_axis=1, concat_axis=2, tiled=True)
    products = jnp.einsum(
        "cim,djm->cdij", row_panel, column_panel, preferred_element_type=jnp.float32
    )
    tile_sum = combine_pairs(products)
    return prior_corr.astype(jnp.float32) + tile_sum


LANES = 128
FRAME = 16
MESH = pl.DeviceIdType.MESH


def quench_kernel(
    row_count, occupied, disorder, region_cols, cheb_coef, out,
    fields, turned, levels, hot, window, picks, operator, product, kept, leaving,
    nearby, crossed, outgoing, incoming, columns, weights,
    here, beside, complete, load_sem, level_send, level_recv, field_send, field_recv,
    near_send, near_recv, cross_send, cross_recv, block_send, block_recv,
):
    r = lax.axis_index("rows")
    o = lax.axis_index("orb")
    g = o % 2
    x = o // 2
    band, width = disorder.shape
    height = band * row_count
    terms = cheb_coef.shape[1]
    reach = terms - 1
    acols = region_cols.shape[0]
    tile = out.shape[1]
    chips = 2 * row_count
    mine = 2 * r + x
    half = row_count // 2
    side = r // half
    place = r % half
    pair = r + 1 - 2 * place
    across = (r + half) % row_count
    owner = g == side
    passer = jnp.logical_not(owner)
    spots = 2 * LANES

    def remote(src, dst, send, recv, row, orb):
        return pltpu.make_async_remote_copy(
            src_ref=src, dst_ref=dst, send_sem=send, recv_sem=recv,
            device_id={"rows": row, "orb": orb}, device_id_type=MESH,
        )

    barrier = pltpu.get_barrier_semaphore()

    def greet(row, orb):
        pl.semaphore_signal(
            barrier, inc=1, device_id={"rows": row, "orb": orb}, device_id_type=MESH
        )

    greet(r, 2 * x + 1 - g)
    for column in range(2, 4):
        pl.when(x == 0)(lambda column=column: greet(r, column))
    for k in range(1, row_count):
        pl.when(r + k < row_count)(lambda k=k: greet((r + k) % row_count, o))

    def chunk(i, which):
        return occupied.at[:, i, :, pl.ds(pl.multiple_of(which * LANES, LANES), LANES)]

    loads = [
        pltpu.make_async_copy(disorder, levels.at[r], load_sem.at[0]),
        pltpu.make_async_copy(region_cols, columns, load_sem.at[1]),
        pltpu.make_async_copy(cheb_coef, weights, load_sem.at[2]),
    ]
    for load in loads:
        load.start()
    def own_load(slot, i):
        return pltpu.make_async_copy(
            chunk(i, place if slot == 0 else 1 - place), fields.at[slot, i], field_recv.at[slot, i]
        )

    for i in range(band):
        own_load(0, i).start()

    @pl.when(owner)
    def _():
        for i in range(band):
            own_load(1, i).start()

    pl.semaphore_wait(barrier, 1 + 2 * x + r)

    def level_copy(slot, kind, row):
        return remote(
            disorder, levels.at[slot], level_send.at[kind], level_recv.at[slot], row, o
        )

    def down(k):
        return level_copy(r, k - 1, (r + row_count - k) % row_count)

    def up(k):
        return level_copy(r, row_count + k - 2, (r + k) % row_count)

    def field_copy(i):
        return remote(
            chunk(i, 1 - place), fields.at[1, i], field_send.at[i],
            field_recv.at[1, i], pair, o,
        )

    def answer(k):
        pl.semaphore_signal(
            here.at[r], inc=1,
            device_id={"rows": (r + row_count - k) % row_count, "orb": o}, device_id_type=MESH,
        )

    def send_fields():
        for i in range(band):
            field_copy(i).start()

    def climb(k):
        pl.semaphore_wait(here.at[(r + k) % row_count], 1)
        up(k).start()

    for k in range(1, row_count):
        pl.when(r >= k)(functools.partial(answer, k))

    def reply(column):
        pl.semaphore_signal(
            beside.at[g], inc=1, device_id={"rows": r, "orb": column}, device_id_type=MESH
        )

    for column in range(2):
        pl.when(x == 1)(functools.partial(reply, column))
    for k in range(row_count - 1, 0, -1):
        pl.when(r >= k)(lambda k=k: down(k).start())
    pl.when(passer & (place == 1))(send_fields)
    pl.when(r + 1 < row_count)(functools.partial(climb, 1))
    pl.when(passer & (place == 0))(send_fields)
    for load in loads:
        load.wait()

    lane = lax.broadcasted_iota(jnp.int32, (1, LANES), 1)
    cols = jnp.zeros((1, LANES), jnp.int32)
    for a in range(acols):
        cols = jnp.where(lane % acols == a, columns[a], cols)
    offset = lax.broadcasted_iota(jnp.int32, (width, LANES), 0) - cols + reach
    offset = jnp.where(offset < 0, offset + width, offset)
    offset = jnp.where(offset >= width, offset - width, offset)
    for d in range(1, 2 * reach):
        hot[d - 1] = jnp.where(offset == d, 1.0, 0.0).astype(jnp.bfloat16)

    first = cols - reach
    first = jnp.where(first < 0, first + width, first)
    first = jnp.concatenate([first, first], axis=1)
    slide = jnp.broadcast_to(first % FRAME, (2 * FRAME, spots))
    strip = jnp.broadcast_to(first // FRAME, (FRAME, spots))
    strips = width // FRAME
    for j in range(strips):
        picks[j] = jnp.where(strip == j, 1.0, 0.0).astype(jnp.bfloat16)

    def turn(slot, i):
        k = band * slot + i
        for part in range(2):
            turned[part * LANES : (part + 1) * LANES, k * width : (k + 1) * width] = (
                fields[slot, i, part].T
            )

    for i in range(band):
        own_load(0, i).wait()
        turn(0, i)

    @pl.when(owner)
    def _():
        for i in range(band):
            own_load(1, i).wait()
            turn(1, i)

    last = row_count - 1

    def both_copy():
        rows = levels.at[pl.ds(0, 2)]
        return remote(rows, rows, level_send.at[row_count], level_recv.at[0], last, o)

    pl.when(r + 2 < last)(functools.partial(climb, 2))

    @pl.when(r == 1)
    def _():
        level_copy(0, 0, last).wait_recv()
        pl.semaphore_wait(here.at[last], 1)
        both_copy().start()

    pl.when(r == 0)(lambda: pl.semaphore_wait(here.at[last], 1))
    for column in range(2):
        pl.when(x == 0)(lambda column=column: pl.semaphore_wait(beside.at[column], 1))
    for k in range(1, row_count):
        pl.semaphore_signal(
            complete.at[r], inc=1,
            device_id={"rows": (r + k) % row_count, "orb": o}, device_id_type=MESH,
        )
    for slot in range(row_count):
        if slot < 2:
            pl.when((r != slot) & (r != last) & ((slot != 0) | (r != 1)))(
                lambda slot=slot: level_copy(slot, 0, last).wait_recv()
            )
        else:
            pl.when(r != slot)(lambda slot=slot: level_copy(slot, 0, last).wait_recv())
    pl.when(r == last)(lambda: both_copy().wait_recv())

    onsite = jnp.concatenate([levels[k] for k in range(row_count)], axis=0)
    onsite = (onsite.astype(jnp.float32) * LEVEL_STEP).astype(jnp.bfloat16)

    local_levels = {}
    for d in range(1, 2 * reach):
        here = jnp.dot(onsite, hot[d - 1], preferred_element_type=jnp.float32)
        local_levels[d] = jnp.concatenate([here, here], axis=1)

    lane = lax.broadcasted_iota(jnp.int32, (height, spots), 1)
    row_id = lax.broadcasted_iota(jnp.int32, (height, spots), 0)
    start = jnp.where(row_id == lane // acols, 1.0, 0.0)
    previous, current = {}, {reach: start}
    real = {reach: weights[0, 0] * start}
    imag = {reach: weights[1, 0] * start}
    for degree in range(1, terms):
        following = {}
        for d in range(reach - degree, reach + degree + 1):
            total = None
            if d in current:
                here = current[d]
                total = local_levels[d] * here - (
                    pltpu.roll(here, 1, 0) + pltpu.roll(here, height - 1, 0)
                )
            for beside in (d - 1, d + 1):
                if beside in current:
                    there = current[beside]
                    total = -there if total is None else total - there
            value = total * ((1.0 if degree == 1 else 2.0) / HOP_SCALE)
            if d in previous:
                value = value - previous[d]
            following[d] = value
            more_real = weights[0, degree] * value
            more_imag = weights[1, degree] * value
            real[d] = real[d] + more_real if d in real else more_real
            imag[d] = imag[d] + more_imag if d in imag else more_imag
        previous, current = current, following
    for part, parts in ((0, real), (1, imag)):
        for d in range(FRAME):
            rows = pl.ds((part * FRAME + d) * height, height)
            value = parts[d] if d in parts else jnp.zeros((height, spots), jnp.float32)
            window[0, rows, :] = value[:, :LANES]
            window[1, rows, :] = value[:, LANES:]

    def expand(slot, i):
        k = band * slot + i
        where = place if slot == 0 else 1 - place
        y = band * (half * side + where) + i
        for part in range(2):
            rows = pl.ds(part * FRAME * height + y, FRAME, stride=height)
            bare = jnp.concatenate([window[0, rows, :], window[1, rows, :]], axis=1)
            frame = jnp.concatenate([bare, jnp.zeros_like(bare)], axis=0)
            step = 1
            while step < FRAME:
                moved = pltpu.roll(frame, step, 0)
                frame = jnp.where((slide & step) != 0, moved, frame)
                step *= 2
            high = frame.astype(jnp.bfloat16)
            low = (frame - high.astype(jnp.float32)).astype(jnp.bfloat16)
            for kind, value in ((0, high), (1, low)):
                upper, lower = value[:FRAME], value[FRAME:]
                for j in range(strips):
                    strip = upper * picks[j] + lower * picks[(j - 1) % strips]
                    rows = slice(k * width + j * FRAME, k * width + (j + 1) * FRAME)
                    for s in range(2):
                        operator[kind, s, rows, part * LANES : (part + 1) * LANES] = strip[
                            :, s * LANES : (s + 1) * LANES
                        ]

    def applied(slot, at, s):
        rows = slice(slot * band * width, (slot + 1) * band * width)
        ats = slice(at * band * width, (at + 1) * band * width)
        return jnp.dot(
            turned[:, rows], operator[0, s, ats, :], preferred_element_type=jnp.float32
        ) + jnp.dot(turned[:, rows], operator[1, s, ats, :], preferred_element_type=jnp.float32)

    def pieces(total):
        return (
            total[:LANES, :LANES] - total[LANES:, LANES:],
            total[LANES:, :LANES] + total[:LANES, LANES:],
        )

    def near_copy(s):
        return remote(
            leaving.at[s], nearby.at[s], near_send.at[s], near_recv.at[s], pair, o
        )

    def cross_copy(s):
        return remote(
            leaving.at[s], crossed.at[s], cross_send.at[s], cross_recv.at[s], across, o
        )

    def leave(s, total, copy):
        parts = pieces(total)
        for part in range(2):
            leaving[s, part] = parts[part].astype(jnp.bfloat16)
        copy(s).start()

    def block_copy(chip, part, slot):
        return remote(
            outgoing.at[2 * chip + part], incoming.at[slot], block_send.at[2 * chip + part],
            block_recv.at[slot], chip // 2, 2 * (chip % 2) + part,
        )

    for k in range(1, row_count):
        pl.semaphore_wait(complete.at[(r + k) % row_count], 1)

    for i in range(band):
        expand(0, i)

    @pl.when(passer)
    def _():
        for s in range(2):
            product[s] = applied(0, 0, s)
        for i in range(band):
            expand(1, i)
        for i in range(band):
            field_copy(i).wait_recv()
            turn(1, i)
        for s in range(2):
            leave(s, product[s] + applied(1, 1, s), cross_copy)

    @pl.when(owner)
    def _():
        for s in range(2):
            parts = pieces(applied(0, 0, s))
            kept[s, 0] = parts[0]
            kept[s, 1] = parts[1]
        for s in range(2):
            leave(s, applied(1, 0, s), near_copy)
        for s in range(2):
            near_copy(s).wait_recv()
            kept[s] = kept[s] + nearby[s].astype(jnp.float32)
        lefts, turns = [], []
        for s in range(2):
            cross_copy(s).wait_recv()
            whole = (kept[s] + crossed[s].astype(jnp.float32)).astype(jnp.bfloat16)
            real_part, imag_part = whole[0].T, whole[1].T
            lefts.append(jnp.concatenate([real_part, imag_part], axis=1))
            turns.append(jnp.concatenate([-imag_part, real_part], axis=1))
        left = jnp.concatenate(lefts, axis=0)
        flipped = jnp.concatenate(turns, axis=0)
        rights = []
        for column in range(4):
            rows = slice(column * tile, (column + 1) * tile)
            rights.append(left[rows])
            rights.append(flipped[rows])
        right = jnp.concatenate(rights, axis=0)
        for turn_of in range(2):
            for row in (0, *range(row_count - 1, 0, -1)):
                blocks = lax.dot_general(
                    left[row * tile : (row + 1) * tile],
                    right[turn_of * 2 * LANES : (turn_of + 1) * 2 * LANES],
                    (((1,), (1,)), ((), ())), preferred_element_type=jnp.float32,
                ).astype(jnp.bfloat16)
                chip = 2 * row + turn_of
                for part in range(2):
                    outgoing[2 * chip + part] = blocks[:, part * LANES : (part + 1) * LANES]
                for part in range(2):

                    @pl.when((mine != chip) | (g != part))
                    def _():
                        block_copy(chip, part, mine).start()

        incoming[mine] = outgoing[2 * mine + g]

    pl.when(passer)(lambda: block_copy(0, 0, mine).wait_recv())
    total = incoming[mine].astype(jnp.float32)
    for k in range(1, chips):
        slot = (mine + chips - k) % chips
        block_copy(0, 0, slot).wait_recv()
        total = total + incoming[slot].astype(jnp.float32)
    out[0] = total[:, :tile]
    out[1] = total[:, tile:]

    for k in range(1, row_count):
        pl.when(r >= k)(lambda k=k: down(k).wait_send())
        if k < 3:
            pl.when(r + k < row_count - (k - 1))(lambda k=k: up(k).wait_send())
    pl.when(r == 1)(lambda: both_copy().wait_send())

    @pl.when(passer)
    def _():
        for i in range(band):
            field_copy(i).wait_send()
        for s in range(2):
            cross_copy(s).wait_send()

    @pl.when(owner)
    def _():
        for s in range(2):
            near_copy(s).wait_send()
        for chip in range(chips):
            for part in range(2):

                @pl.when((mine != chip) | (g != part))
                def _():
                    block_copy(chip, part, mine).wait_send()


def fused_step(row_count, occupied, disorder, region_cols, cheb_coef, prior_corr):
    band, width = disorder.shape
    terms = cheb_coef.shape[1]
    tile = prior_corr.shape[1]
    height = band * row_count
    chips = 2 * row_count
    half = row_count // 2
    spots = 2 * LANES
    dma = pltpu.SemaphoreType.DMA
    anywhere = pl.BlockSpec(memory_space=pl.ANY)
    corr = pl.pallas_call(
        functools.partial(quench_kernel, row_count),
        out_shape=pltpu.VMEM(prior_corr.shape, jnp.float32),
        in_specs=[anywhere] * 4,
        out_specs=pl.BlockSpec(memory_space=pltpu.VMEM),
        scratch_shapes=[
            pltpu.VMEM((2, band, 2, width, LANES), jnp.bfloat16),
            pltpu.VMEM((2 * LANES, height // 2 * width), jnp.bfloat16),
            pltpu.VMEM((row_count, band, width), jnp.int32),
            pltpu.VMEM((2 * terms - 3, width, LANES), jnp.bfloat16),
            pltpu.VMEM((2, 2 * FRAME * height, LANES), jnp.float32),
            pltpu.VMEM((width // FRAME, FRAME, spots), jnp.bfloat16),
            pltpu.VMEM((2, 2, height // 2 * width, spots), jnp.bfloat16),
            pltpu.VMEM((2, 2 * LANES, spots), jnp.float32),
            pltpu.VMEM((2, 2, LANES, LANES), jnp.float32),
            pltpu.VMEM((2, 2, LANES, LANES), jnp.bfloat16),
            pltpu.VMEM((2, 2, LANES, LANES), jnp.bfloat16),
            pltpu.VMEM((2, 2, LANES, LANES), jnp.bfloat16),
            pltpu.VMEM((2 * chips, tile, LANES), jnp.bfloat16),
            pltpu.VMEM((chips, tile, LANES), jnp.bfloat16),
            pltpu.SMEM(region_cols.shape, jnp.int32),
            pltpu.SMEM(cheb_coef.shape, jnp.float32),
            pltpu.SemaphoreType.REGULAR((row_count,)),
            pltpu.SemaphoreType.REGULAR((2,)),
            pltpu.SemaphoreType.REGULAR((row_count,)),
            dma((3,)),
            dma((2 * row_count - 2,)),
            dma((row_count,)),
            dma((band,)),
            dma((2, band)),
            dma((2,)),
            dma((2,)),
            dma((2,)),
            dma((2,)),
            dma((2 * chips,)),
            dma((chips,)),
        ],
        compiler_params=pltpu.CompilerParams(collective_id=0, has_side_effects=True),
    )(occupied, disorder, region_cols, cheb_coef)
    return prior_corr.astype(jnp.float32) + corr


def local_step(row_count, orb_count, occupied, disorder, region_cols, cheb_coef, prior_corr):
    band, width, orbitals = occupied.shape[1:]
    terms = cheb_coef.shape[1]
    height = band * row_count
    sites = height * region_cols.shape[0]
    fused = (
        orb_count == 4
        and row_count == 4
        and sites == 2 * LANES
        and 2 * orbitals == row_count * LANES
        and orbitals == 2 * LANES
        and height % 8 == 0
        and width % LANES == 0
        and width >= 2 * FRAME
        and 2 * terms <= FRAME
        and LANES % region_cols.shape[0] == 0
        and prior_corr.shape[1:] == (LANES // 2, LANES // 2)
    )
    if fused:
        return fused_step(row_count, occupied, disorder, region_cols, cheb_coef, prior_corr)
    return shards(occupied, disorder, region_cols, cheb_coef, prior_corr)


def solution(mesh):
    return jax.shard_map(
        functools.partial(local_step, mesh.shape["rows"], mesh.shape["orb"]),
        mesh=mesh,
        in_specs=(
            P(None, ("real", "rows"), None, "orb"),
            P(("real", "rows"), None),
            P(),
            P(),
            P(None, ("real", "rows"), "orb"),
        ),
        out_specs=P(None, ("real", "rows"), "orb"),
        check_vma=False,
    )
```
